32 devices in a mesh: row: 8 (over y, x, core), col: 4 (over z).
Axes of the slice: x: 2, y: 2, z: 4, core: 2. Of those that a mesh axis runs over, the one named last changes fastest.
Arguments:
- coeffs: bfloat16 [16384, 2048], P('row', 'col'), may hold values from -0.8984375 to 0.8984375
- occupations: float32 [2048], replicated, may hold values from 0.05 to 2
- block_order: int32 [32], replicated, may hold values from 0 to 31, as said below
- neighbours: int32 [32, 15], P(('row', 'col')), may hold values from 0 to 31, as said below
- counts: int32 [32], P(('row', 'col')), may hold values from 4 to 15, as said below
Outputs:
- density: bfloat16 [32, 15, 512, 512], P(('row', 'col'))
The draws below stay inside these ranges and needn't reach their ends.
Inputs may be any that keep to these rules, and one draw needn't show every extreme that they name: Within each aligned group of 4 entries, block_order is a permutation of that group's own indices. For atom row block a, the first counts[a] entries of neighbours[a] are distinct blocks b with |b - a| < 8; the remaining entries equal a. `counts`: some block has 15 live slots in every draw.
All inputs are finite; a program needn't handle non-finite values.
Results may differ from the reference program's by a relative error of at most 0.0044.
Values may be sent and summed in bfloat16 or wider, within the bound.
A program may use at most 128 MiB of HBM per device.

```python
import jax
import jax.numpy as jnp
from jax import lax

BS = 512
STATES = 2048
W = 8
NNB = 15
NBLK = 32
NB = 16384
N_COL = 4


def pattern_draw(key):
    base = jax.random.fold_in(key, 71)
    offsets = jnp.arange(NNB, dtype=jnp.int32) - (W - 1)
    row_keys = jax.random.split(jax.random.fold_in(base, 1), NBLK)
    shuffled = jax.vmap(lambda k: jax.random.permutation(k, offsets))(row_keys)
    blocks = jnp.arange(NBLK, dtype=jnp.int32)
    targets = blocks[:, None] + shuffled
    valid = (targets >= 0) & (targets < NBLK) & (shuffled != 0)
    ranks = jnp.argsort(jnp.where(valid, 0, 1).astype(jnp.int32), axis=1, stable=True)
    targets = jnp.take_along_axis(targets, ranks, axis=1)
    available = jnp.sum(valid.astype(jnp.int32), axis=1) + 1
    wanted = jax.random.randint(jax.random.fold_in(base, 2), (NBLK,), 4, NNB + 1).astype(jnp.int32)
    heavy = jax.random.randint(jax.random.fold_in(base, 3), (), W, NBLK - W + 1).astype(jnp.int32)
    wanted = jnp.where(blocks == heavy, NNB, wanted)
    live = jnp.minimum(wanted, available)
    own_first = jnp.concatenate([blocks[:, None], targets[:, :NNB - 1]], axis=1)
    slots = jnp.arange(NNB, dtype=jnp.int32)[None, :]
    lists = jnp.where(slots < live[:, None], own_first, blocks[:, None])
    return (lists.astype(jnp.int32), live.astype(jnp.int32))


def draw_neighbours(key, part):
    return pattern_draw(key)[0]


def draw_counts(key, part):
    return pattern_draw(key)[1]


def draw_block_order(key, part):
    group_keys = jax.random.split(jax.random.fold_in(key, 5), NBLK // N_COL)
    perms = jax.vmap(lambda k: jax.random.permutation(k, N_COL))(group_keys).astype(jnp.int32)
    bases = (jnp.arange(NBLK // N_COL, dtype=jnp.int32) * N_COL)[:, None]
    return (perms + bases).reshape(NBLK).astype(jnp.int32)


def level_of(key, shape, shards, smallest, high):
    def one(position, shards_of):
        heights = jax.random.uniform(jax.random.fold_in(jax.random.fold_in(key, 6), position), (shards_of,), jnp.float32, smallest / len(shards), high / len(shards))
        return jnp.repeat(jnp.exp(heights), shape[position] // shards_of).reshape((-1,) + (1,) * (len(shape) - position - 1))

    factor_of = one(*shards[0])
    for cut in shards[1:]:
        factor_of = factor_of * one(*cut)
    return factor_of


def noise(key, extent, scale, bound, cuts=(), kind=jnp.bfloat16):
    values = scale * jax.random.normal(key, extent, jnp.float32)
    if cuts:
        values = values * level_of(key, extent, cuts, -0.22, 0.18)
    return jnp.clip(values, -bound, bound).astype(kind)


def setup_inputs(seed: int = 0) -> dict:
    keys = jax.random.split(jax.random.key(seed), 6)
    coeffs = noise(keys[0], (NB, STATES), 0.15, 0.8984375, ((0, 8), (1, 4)))
    occupations = jnp.clip(jax.random.uniform(keys[1], (STATES,), jnp.float32, 0.05, 2.0), 0.05, 2.0)
    block_order = draw_block_order(jax.random.fold_in(keys[5], 71), 0)
    neighbours = draw_neighbours(jax.random.fold_in(keys[5], 71), 0)
    counts = draw_counts(jax.random.fold_in(keys[5], 71), 0)
    return dict(coeffs=coeffs, occupations=occupations, block_order=block_order, neighbours=neighbours, counts=counts)


def reference(coeffs, occupations, block_order, neighbours, counts):
    atoms = coeffs.reshape(NBLK, BS, STATES)[block_order.astype(jnp.int32)]
    weighted = (atoms.astype(jnp.float32) * occupations[None, None, :]).astype(jnp.bfloat16)
    slots = jnp.arange(NNB, dtype=jnp.int32)

    def one_block(items):
        weight_rows, partner, live_count = items
        chosen = atoms[partner.astype(jnp.int32)].astype(jnp.float32)
        products = jnp.einsum("ik,jnk->jin", weight_rows.astype(jnp.float32), chosen)
        live = (slots < live_count)[:, None, None]
        return jnp.where(live, products, jnp.zeros_like(products)).astype(jnp.bfloat16)

    return lax.map(one_block, (weighted, neighbours, counts))
```

```python
import functools

import jax
import jax.numpy as jnp
from jax import lax
from jax.experimental import pallas as pl
from jax.experimental.pallas import tpu as pltpu
from jax.sharding import PartitionSpec as P

W = 8
MESH = pl.DeviceIdType.MESH


def kernel(rows, cols, per, own_ref, occ_ref, out_ref, gat, wgt, res, in_sem, dsem, fsem, psem, rsem, xsem, usem, osem, qsem):
    row, z = lax.axis_index("row"), lax.axis_index("col")
    k = lax.rem(row, per)
    base = row - k
    place = k * cols + z
    size = per * cols
    has_up, has_down = row + per < rows, row >= per

    def remote(src, dst, send, recv, device):
        return pltpu.make_async_remote_copy(
            src_ref=src, dst_ref=dst, send_sem=send, recv_sem=recv, device_id=device, device_id_type=MESH
        )

    def direct(i):
        return remote(gat.at[k, i, z], gat.at[k, i, z], dsem.at[i], rsem.at[k, i, z], (row, i))

    def onward(way, i, c):
        step = 1 - 2 * way
        there = lax.rem(z + step + cols, cols)
        return remote(gat.at[k, i, c], gat.at[k, i, c], fsem.at[way, i, c], rsem.at[k, i, c], (row, there))

    def partner(d, i, c):
        there = base + lax.rem(k + d, per)
        return remote(gat.at[k, i, c], gat.at[k, i, c], psem.at[d - 1, i, c], rsem.at[k, i, c], (there, z))

    def ship(way, c):
        there = lax.rem(row + (1 - 2 * way) * per + rows, rows)
        return remote(gat.at[k, z, c], wgt.at[way, c], xsem.at[way, c], usem.at[way, c], (there, z))

    def arrive(kk, i, c):
        remote(gat.at[kk, i, c], gat.at[kk, i, c], dsem.at[0], rsem.at[kk, i, c], (row, z)).wait_recv()

    def pass_on(i, c, act):
        @pl.when((c <= z) & (z < cols - 1) & (i != z + 1))
        def _():
            act(onward(0, i, c))

        @pl.when((c >= z) & (z > 0) & (i != z - 1))
        def _():
            act(onward(1, i, c))

        for d in range(1, per):
            act(partner(d, i, c))

    def ship_on(c, act):
        @pl.when(has_up)
        def _():
            act(ship(0, c))

        @pl.when(has_down)
        def _():
            act(ship(1, c))

    def start(copy):
        copy.start()

    def sent(copy):
        copy.wait_send()

    fill = pltpu.make_async_copy(own_ref, gat.at[k, :, z], in_sem)
    fill.start()
    barrier = pltpu.get_barrier_semaphore()
    for d in range(1, cols):
        pl.semaphore_signal(barrier, inc=1, device_id=(row, lax.rem(z + d, cols)), device_id_type=MESH)
    for d in range(1, per):
        pl.semaphore_signal(barrier, inc=1, device_id=(base + lax.rem(k + d, per), z), device_id_type=MESH)

    @pl.when(has_up)
    def _():
        pl.semaphore_signal(barrier, inc=1, device_id=(lax.rem(row + per, rows), z), device_id_type=MESH)

    @pl.when(has_down)
    def _():
        pl.semaphore_signal(barrier, inc=1, device_id=(lax.rem(row - per + rows, rows), z), device_id_type=MESH)

    pl.semaphore_wait(barrier, cols + per - 2 + has_up.astype(jnp.int32) + has_down.astype(jnp.int32))
    fill.wait()

    for d in range(1, cols):
        direct(lax.rem(z + d, cols)).start()
    ship_on(z, start)

    @pl.loop(0, cols)
    def _(i):
        pass_on(i, z, start)

    def sides(s, act):
        @pl.when(z - s >= 0)
        def _():
            act(z - s)

        @pl.when(z + s < cols)
        def _():
            act(z + s)

    @pl.loop(1, cols)
    def _(s):
        def act(c):
            arrive(k, z, c)
            ship_on(c, start)
            pass_on(z, c, start)

        sides(s, act)

    @pl.loop(0, cols)
    def _(i):
        @pl.when(i != z)
        def _():
            @pl.loop(1, cols)
            def _(s):
                def act(c):
                    arrive(k, i, c)
                    pass_on(i, c, start)

                sides(s, act)

    def scale(way, source):
        @pl.loop(0, cols)
        def _(c):
            wgt[way, c] = (source(c).astype(jnp.float32) * occ_ref[c]).astype(jnp.bfloat16)

    for way, present in ((0, has_down), (1, has_up)):

        @pl.when(present)
        def _():
            @pl.loop(0, cols)
            def _(c):
                remote(wgt.at[way, c], wgt.at[way, c], dsem.at[0], usem.at[way, c], (row, z)).wait_recv()

            scale(way, lambda c: wgt[way, c])

    scale(2, lambda c: gat[k, z, c])
    for d in range(1, per):
        kk = lax.rem(k + d, per)

        @pl.loop(0, cols)
        def _(i):
            @pl.loop(0, cols)
            def _(c):
                arrive(kk, i, c)

    def answer(t):
        low = t < place
        other = jnp.where(low, t, t + 1)
        slot = jnp.where(low, size + other - place, other - place - size) + W - 1
        near = (slot >= 0) & (slot < 2 * W - 1)
        return low, other, slot, near

    def reply(t):
        low, other, slot, near = answer(t)
        there = lax.rem(jnp.where(low, row - per, row + per) + rows, rows)
        go = near & jnp.where(low, row - per >= 0, row + per < rows)
        slot = jnp.clip(slot, 0, 2 * W - 2)
        return go, remote(res.at[t], out_ref.at[slot], osem.at[t], qsem.at[slot], (there, z))

    def local(t):
        other = t - (size - 1)
        slot = other - place + W - 1
        near = (slot >= 0) & (slot < 2 * W - 1)
        slot = jnp.clip(slot, 0, 2 * W - 2)
        return near, pltpu.make_async_copy(res.at[t], out_ref.at[slot], osem.at[t])

    def product(t, way, other):
        kk, i = other // cols, lax.rem(other, cols)
        total = jnp.zeros(res.shape[1:], jnp.float32)
        for c in range(cols):
            total = total + lax.dot_general(
                wgt[way, c], gat[kk, i, c], (((1,), (1,)), ((), ())), preferred_element_type=jnp.float32
            )
        res[t] = total.astype(jnp.bfloat16)

    @pl.loop(0, size - 1)
    def _(t):
        go, copy = reply(t)
        low, other, _, _ = answer(t)

        @pl.when(go)
        def _():
            product(t, jnp.where(low, 0, 1), other)
            copy.start()

    @pl.loop(size - 1, 2 * size - 1)
    def _(t):
        near, copy = local(t)

        @pl.when(near)
        def _():
            product(t, 2, t - (size - 1))
            copy.start()

    for d in range(1, cols):
        direct(lax.rem(z + d, cols)).wait_send()

    @pl.loop(0, cols)
    def _(c):
        ship_on(c, sent)

        @pl.loop(0, cols)
        def _(i):
            pass_on(i, c, sent)

    @pl.loop(0, size - 1)
    def _(t):
        go, copy = reply(t)

        @pl.when(go)
        def _():
            copy.wait_send()

        low, other, slot, near = answer(t)
        due = near & jnp.where(low, row + per < rows, row - per >= 0)
        slot = jnp.clip(slot, 0, 2 * W - 2)

        @pl.when(due)
        def _():
            remote(res.at[t], out_ref.at[slot], osem.at[t], qsem.at[slot], (row, z)).wait_recv()

    @pl.loop(size - 1, 2 * size - 1)
    def _(t):
        near, copy = local(t)

        @pl.when(near)
        def _():
            copy.wait()


def shards(coeffs, occupations, block_order, neighbours, counts):
    rows, cols = lax.axis_size("row"), lax.axis_size("col")
    states = coeffs.shape[1]
    depth = coeffs.shape[0] // cols
    per = -(-W // cols)
    size = per * cols
    slots_total = 2 * W - 1
    first = lax.axis_index("row") * cols
    picks = lax.dynamic_slice_in_dim(block_order, first, cols) - first
    own = coeffs.reshape(cols, depth, states)[picks]
    occ = occupations.reshape(cols, 1, states)
    dma = pltpu.SemaphoreType.DMA
    blocks = pl.pallas_call(
        functools.partial(kernel, rows, cols, per),
        out_shape=jax.ShapeDtypeStruct((slots_total, depth, depth), jnp.bfloat16),
        in_specs=[pl.BlockSpec(memory_space=pl.ANY), pl.BlockSpec(memory_space=pltpu.VMEM)],
        out_specs=pl.BlockSpec(memory_space=pl.ANY),
        scratch_shapes=[
            pltpu.VMEM((per, cols, cols, depth, states), jnp.bfloat16),
            pltpu.VMEM((3, cols, depth, states), jnp.bfloat16),
            pltpu.VMEM((2 * size - 1, depth, depth), jnp.bfloat16),
            dma,
            dma((cols,)),
            dma((2, cols, cols)),
            dma((max(per - 1, 1), cols, cols)),
            dma((per, cols, cols)),
            dma((2, cols)),
            dma((2, cols)),
            dma((2 * size - 1,)),
            dma((slots_total,)),
        ],
        compiler_params=pltpu.CompilerParams(
            collective_id=0, has_side_effects=True, vmem_limit_bytes=60 * 1024 * 1024
        ),
        name="density_blocks",
    )(own, occ)
    here = first + lax.axis_index("col")
    offsets = neighbours[0] - here + (W - 1)
    live = jnp.arange(neighbours.shape[1], dtype=jnp.int32) < counts[0]
    return jnp.where(live[:, None, None], blocks[offsets], 0)[None]


def solution(mesh):
    return jax.shard_map(
        shards,
        mesh=mesh,
        in_specs=(P("row", "col"), P(), P(), P(("row", "col"), None), P(("row", "col"))),
        out_specs=P(("row", "col"), None, None, None),
        check_vma=False,
    )
```

```python
import functools

import jax
import jax.numpy as jnp
from jax import lax
from jax.experimental import pallas as pl
from jax.experimental.pallas import tpu as pltpu
from jax.sharding import PartitionSpec as P

W = 8
LAG = 2
MESH = pl.DeviceIdType.MESH


def kernel(rows, cols, per, own_ref, occ_ref, out_ref, gat, raw, wgt, res, in_sem, dsem, fsem, psem, rsem, xsem, ysem, usem, osem, qsem):
    row, z = lax.axis_index("row"), lax.axis_index("col")
    k = lax.rem(row, per)
    base = row - k
    place = k * cols + z
    size = per * cols
    has_up, has_down = row + per < rows, row >= per
    has_up2, has_down2 = row + 2 * per < rows, row >= 2 * per
    odd = lax.rem(row // per, 2) == 1
    ships_up = has_up & jnp.logical_not(odd) & ((place > 0) | has_down)
    ships_down = has_down & jnp.where(odd, (place < size - 1) | has_up, (place < size - 1) & jnp.logical_not(has_up))
    relays_up = has_up2 & (place > 0) & jnp.logical_not(odd)
    relays_down = has_down2 & (place < size - 1) & odd
    lower, upper = has_down & (place > 0), has_up & (place < size - 1)
    edge = (z == 0) | (z == cols - 1)

    def remote(src, dst, send, recv, device):
        return pltpu.make_async_remote_copy(
            src_ref=src, dst_ref=dst, send_sem=send, recv_sem=recv, device_id=device, device_id_type=MESH
        )

    def direct(i):
        return remote(gat.at[k, i, z], gat.at[k, i, z], dsem.at[i], rsem.at[k, i, z], (row, i))

    def onward(way, i, c):
        step = 1 - 2 * way
        there = lax.rem(z + step + cols, cols)
        return remote(gat.at[k, i, c], gat.at[k, i, c], fsem.at[way, i, c], rsem.at[k, i, c], (row, there))

    def partner(d, i, c):
        there = base + lax.rem(k + d, per)
        return remote(gat.at[k, i, c], gat.at[k, i, c], psem.at[d - 1, i, c], rsem.at[k, i, c], (there, z))

    def ship(way, c):
        there = lax.rem(row + (1 - 2 * way) * per + rows, rows)
        return remote(gat.at[k, z, c], raw.at[way, c], xsem.at[way, c], usem.at[way, c], (there, z))

    def relay(way, c):
        there = lax.rem(row + (2 - 4 * way) * per + 2 * rows, rows)
        return remote(raw.at[1 - way, c], raw.at[way, c], ysem.at[c], usem.at[way, c], (there, z))

    def taken(way, c):
        remote(raw.at[way, c], raw.at[way, c], xsem.at[0, 0], usem.at[way, c], (row, z)).wait_recv()

    def arrive(kk, i, c):
        remote(gat.at[kk, i, c], gat.at[kk, i, c], dsem.at[0], rsem.at[kk, i, c], (row, z)).wait_recv()

    def pass_on(i, c, act):
        @pl.when((c <= z) & (z < cols - 1) & (i != z + 1))
        def _():
            act(onward(0, i, c))

        @pl.when((c >= z) & (z > 0) & (i != z - 1))
        def _():
            act(onward(1, i, c))

        for d in range(1, per):
            act(partner(d, i, c))

    def ship_on(c, act):
        @pl.when(ships_up)
        def _():
            act(ship(0, c))

        @pl.when(ships_down)
        def _():
            act(ship(1, c))

    def start(copy):
        copy.start()

    def sent(copy):
        copy.wait_send()

    fill = pltpu.make_async_copy(own_ref, gat.at[k, :, z], in_sem)
    fill.start()
    barrier = pltpu.get_barrier_semaphore()
    for d in range(1, cols):
        pl.semaphore_signal(barrier, inc=1, device_id=(row, lax.rem(z + d, cols)), device_id_type=MESH)
    for d in range(1, per):
        pl.semaphore_signal(barrier, inc=1, device_id=(base + lax.rem(k + d, per), z), device_id_type=MESH)

    greeted = cols + per - 2
    for present, step in ((has_up, per), (has_down, -per), (has_up2, 2 * per), (has_down2, -2 * per)):
        greeted = greeted + present.astype(jnp.int32)

        @pl.when(present)
        def _():
            there = lax.rem(row + step + 2 * rows, rows)
            pl.semaphore_signal(barrier, inc=1, device_id=(there, z), device_id_type=MESH)

    pl.semaphore_wait(barrier, greeted)
    fill.wait()

    for d in range(1, cols):
        direct(lax.rem(z + d, cols)).start()
    ship_on(z, start)

    @pl.loop(0, cols)
    def _(i):
        pass_on(i, z, start)

    def sides(s, act):
        @pl.when(z - s >= 0)
        def _():
            act(z - s)

        @pl.when(z + s < cols)
        def _():
            act(z + s)

    @pl.loop(1, cols)
    def _(s):
        def act(c):
            arrive(k, z, c)
            ship_on(c, start)
            pass_on(z, c, start)

        sides(s, act)

    def relay_on(c, act):
        @pl.when(relays_up)
        def _():
            act(relay(0, c), 1)

        @pl.when(relays_down)
        def _():
            act(relay(1, c), 0)

    def receive_and_relay(c):
        def act(copy, way):
            taken(way, c)
            copy.start()

        relay_on(c, act)

    receive_and_relay(z)

    @pl.loop(1, cols)
    def _(s):
        sides(s, receive_and_relay)

    def scale(way, source):
        @pl.loop(0, cols)
        def _(c):
            wgt[way, c] = (source(c).astype(jnp.float32) * occ_ref[c]).astype(jnp.bfloat16)

    def prepare():
        for way, present, waited in ((0, lower, relays_down), (1, upper, relays_up)):

            @pl.when(present)
            def _():
                @pl.when(jnp.logical_not(waited))
                def _():
                    @pl.loop(0, cols)
                    def _(c):
                        taken(way, c)

                scale(way, lambda c: raw[way, c])

        scale(2, lambda c: gat[k, z, c])

    def answer(t):
        low = t < place
        other = jnp.where(low, t, t + 1)
        slot = jnp.where(low, size + other - place, other - place - size) + W - 1
        near = (slot >= 0) & (slot < 2 * W - 1)
        return low, other, slot, near

    def reply(t):
        low, other, slot, near = answer(t)
        there = lax.rem(jnp.where(low, row - per, row + per) + rows, rows)
        go = near & jnp.where(low, row - per >= 0, row + per < rows)
        slot = jnp.clip(slot, 0, 2 * W - 2)
        return go, remote(res.at[t], out_ref.at[slot], osem.at[t], qsem.at[slot], (there, z))

    def local(t):
        other = t - (size - 1)
        slot = other - place + W - 1
        near = (slot >= 0) & (slot < 2 * W - 1)
        slot = jnp.clip(slot, 0, 2 * W - 2)
        return near, pltpu.make_async_copy(res.at[t], out_ref.at[slot], osem.at[t])

    def product(t, way, other):
        kk, i = other // cols, lax.rem(other, cols)
        total = jnp.zeros(res.shape[1:], jnp.float32)
        for c in range(cols):
            total = total + lax.dot_general(
                wgt[way, c], gat[kk, i, c], (((1,), (1,)), ((), ())), preferred_element_type=jnp.float32
            )
        res[t] = total.astype(jnp.bfloat16)

    def home(other):
        t = other + size - 1
        near, copy = local(t)

        @pl.when(near)
        def _():
            product(t, 2, other)
            copy.start()

    def away(other):
        low = other < place
        t = jnp.clip(jnp.where(low, other, other - 1), 0, size - 2)
        go, copy = reply(t)

        @pl.when(go & (other != place))
        def _():
            product(t, jnp.where(low, 0, 1), other)
            copy.start()

    def work(q):
        i = jnp.where(q == 0, z, jnp.where(q - 1 < z, q - 1, q))
        for d in range(1, per):
            kk = lax.rem(k + d, per)

            @pl.loop(0, cols)
            def _(c):
                arrive(kk, i, c)

        @pl.loop(0, per)
        def _(kk):
            away(kk * cols + i)

        @pl.when(edge)
        def _():
            @pl.loop(0, per)
            def _(kk):
                home(kk * cols + i)

    lag = jnp.where(edge, 0, LAG)

    @pl.loop(0, cols + LAG)
    def _(n):
        @pl.when((n >= 1) & (n < cols))
        def _():
            i = jnp.where(n - 1 < z, n - 1, n)

            @pl.loop(1, cols)
            def _(s):
                def act(c):
                    arrive(k, i, c)
                    pass_on(i, c, start)

                sides(s, act)

        q = n - lag

        @pl.when(q == 0)
        def _():
            prepare()

        @pl.when((q >= 0) & (q < cols))
        def _():
            work(q)

    @pl.when(jnp.logical_not(edge))
    def _():
        @pl.loop(0, size)
        def _(other):
            home(other)

    for d in range(1, cols):
        direct(lax.rem(z + d, cols)).wait_send()

    @pl.loop(0, cols)
    def _(c):
        ship_on(c, sent)
        relay_on(c, lambda copy, way: sent(copy))

        @pl.loop(0, cols)
        def _(i):
            pass_on(i, c, sent)

    @pl.loop(0, size - 1)
    def _(t):
        go, copy = reply(t)

        @pl.when(go)
        def _():
            copy.wait_send()

        low, other, slot, near = answer(t)
        due = near & jnp.where(low, row + per < rows, row - per >= 0)
        slot = jnp.clip(slot, 0, 2 * W - 2)

        @pl.when(due)
        def _():
            remote(res.at[t], out_ref.at[slot], osem.at[t], qsem.at[slot], (row, z)).wait_recv()

    @pl.loop(size - 1, 2 * size - 1)
    def _(t):
        near, copy = local(t)

        @pl.when(near)
        def _():
            copy.wait()


def place_blocks(at_ref, live_ref, block_ref, out_ref):
    live = live_ref[pl.program_id(0)] > 0

    @pl.when(live)
    def _():
        out_ref[...] = block_ref[...]

    @pl.when(jnp.logical_not(live))
    def _():
        out_ref[...] = jnp.zeros_like(out_ref)


def shards(coeffs, occupations, block_order, neighbours, counts):
    rows, cols = lax.axis_size("row"), lax.axis_size("col")
    states = coeffs.shape[1]
    depth = coeffs.shape[0] // cols
    per = -(-W // cols)
    size = per * cols
    slots_total = 2 * W - 1
    first = lax.axis_index("row") * cols
    picks = lax.dynamic_slice_in_dim(block_order, first, cols) - first
    own = coeffs.reshape(cols, depth, states)[picks]
    occ = occupations.reshape(cols, 1, states)
    dma = pltpu.SemaphoreType.DMA
    blocks = pl.pallas_call(
        functools.partial(kernel, rows, cols, per),
        out_shape=jax.ShapeDtypeStruct((slots_total, depth, depth), jnp.bfloat16),
        in_specs=[pl.BlockSpec(memory_space=pl.ANY), pl.BlockSpec(memory_space=pltpu.VMEM)],
        out_specs=pl.BlockSpec(memory_space=pl.ANY),
        scratch_shapes=[
            pltpu.VMEM((per, cols, cols, depth, states), jnp.bfloat16),
            pltpu.VMEM((2, cols, depth, states), jnp.bfloat16),
            pltpu.VMEM((3, cols, depth, states), jnp.bfloat16),
            pltpu.VMEM((2 * size - 1, depth, depth), jnp.bfloat16),
            dma,
            dma((cols,)),
            dma((2, cols, cols)),
            dma((max(per - 1, 1), cols, cols)),
            dma((per, cols, cols)),
            dma((2, cols)),
            dma((cols,)),
            dma((2, cols)),
            dma((2 * size - 1,)),
            dma((slots_total,)),
        ],
        compiler_params=pltpu.CompilerParams(
            collective_id=0, has_side_effects=True, vmem_limit_bytes=60 * 1024 * 1024
        ),
        name="density_blocks",
    )(own, occ)
    here = first + lax.axis_index("col")
    offsets = neighbours[0] - here + (W - 1)
    live = jnp.arange(neighbours.shape[1], dtype=jnp.int32) < counts[0]
    plan = pltpu.PrefetchScalarGridSpec(
        num_scalar_prefetch=2,
        grid=(offsets.shape[0],),
        in_specs=[pl.BlockSpec((1, depth, depth), lambda j, at, live: (at[j], 0, 0))],
        out_specs=pl.BlockSpec((1, depth, depth), lambda j, at, live: (j, 0, 0)),
    )
    return pl.pallas_call(
        place_blocks,
        grid_spec=plan,
        out_shape=jax.ShapeDtypeStruct((offsets.shape[0], depth, depth), jnp.bfloat16),
        name="place_blocks",
    )(offsets, live.astype(jnp.int32), blocks)[None]


def solution(mesh):
    return jax.shard_map(
        shards,
        mesh=mesh,
        in_specs=(P("row", "col"), P(), P(), P(("row", "col"), None), P(("row", "col"))),
        out_specs=P(("row", "col"), None, None, None),
        check_vma=False,
    )
```

```python
import functools

import jax
import jax.numpy as jnp
from jax import lax
from jax.experimental import pallas as pl
from jax.experimental.pallas import tpu as pltpu
from jax.sharding import PartitionSpec as P

W = 8
MESH = pl.DeviceIdType.MESH


def kernel(rows, cols, per, own_ref, occ_ref, out_ref, gat, raw, wgt, res, in_sem, fsem, psem, rsem, xsem, ysem, usem, osem, qsem):
    row, z = lax.axis_index("row"), lax.axis_index("col")
    k = lax.rem(row, per)
    base = row - k
    place = k * cols + z
    size = per * cols
    has_up, has_down = row + per < rows, row >= per
    has_up2, has_down2 = row + 2 * per < rows, row >= 2 * per
    odd = lax.rem(row // per, 2) == 1
    ships_up = has_up & jnp.logical_not(odd) & ((place > 0) | has_down)
    ships_down = has_down & jnp.where(odd, (place < size - 1) | has_up, (place < size - 1) & jnp.logical_not(has_up))
    relays_up = has_up2 & (place > 0) & jnp.logical_not(odd)
    relays_down = has_down2 & (place < size - 1) & odd
    lower, upper = has_down & (place > 0), has_up & (place < size - 1)
    edge = (z == 0) | (z == cols - 1)

    def remote(src, dst, send, recv, device):
        return pltpu.make_async_remote_copy(
            src_ref=src, dst_ref=dst, send_sem=send, recv_sem=recv, device_id=device, device_id_type=MESH
        )

    def onward(way, i, c):
        step = 1 - 2 * way
        there = lax.rem(z + step + cols, cols)
        return remote(gat.at[k, i, c], gat.at[k, i, c], fsem.at[way, i, c], rsem.at[k, i, c], (row, there))

    def partner(d, i, c):
        there = base + lax.rem(k + d, per)
        return remote(gat.at[k, i, c], gat.at[k, i, c], psem.at[d - 1, i, c], rsem.at[k, i, c], (there, z))

    def ship(way, c):
        there = lax.rem(row + (1 - 2 * way) * per + rows, rows)
        return remote(gat.at[k, z, c], raw.at[way, c], xsem.at[way, c], usem.at[way, c], (there, z))

    def relay(way, c):
        there = lax.rem(row + (2 - 4 * way) * per + 2 * rows, rows)
        return remote(raw.at[1 - way, c], raw.at[way, c], ysem.at[c], usem.at[way, c], (there, z))

    def taken(way, c):
        remote(raw.at[way, c], raw.at[way, c], xsem.at[0, 0], usem.at[way, c], (row, z)).wait_recv()

    def arrive(kk, i, c):
        remote(gat.at[kk, i, c], gat.at[kk, i, c], psem.at[0, 0, 0], rsem.at[kk, i, c], (row, z)).wait_recv()

    def onward_on(way, i, c, act):
        @pl.when(jnp.where(way == 0, (c <= z) & (z < cols - 1), (c >= z) & (z > 0)))
        def _():
            act(onward(way, i, c))

    def partner_on(i, c, act):
        for d in range(1, per):
            act(partner(d, i, c))

    def ship_on(c, act):
        @pl.when(ships_up)
        def _():
            act(ship(0, c))

        @pl.when(ships_down)
        def _():
            act(ship(1, c))

    def start(copy):
        copy.start()

    def sent(copy):
        copy.wait_send()

    fill = pltpu.make_async_copy(own_ref, gat.at[k, :, z], in_sem)
    fill.start()
    barrier = pltpu.get_barrier_semaphore()
    for d in range(1, cols):
        pl.semaphore_signal(barrier, inc=1, device_id=(row, lax.rem(z + d, cols)), device_id_type=MESH)
    for d in range(1, per):
        pl.semaphore_signal(barrier, inc=1, device_id=(base + lax.rem(k + d, per), z), device_id_type=MESH)

    greeted = cols + per - 2
    for present, step in ((has_up, per), (has_down, -per), (has_up2, 2 * per), (has_down2, -2 * per)):
        greeted = greeted + present.astype(jnp.int32)

        @pl.when(present)
        def _():
            there = lax.rem(row + step + 2 * rows, rows)
            pl.semaphore_signal(barrier, inc=1, device_id=(there, z), device_id_type=MESH)

    pl.semaphore_wait(barrier, greeted)
    fill.wait()

    def stream(way, i, s):
        c = z - s if way == 0 else z + s

        @pl.when((c >= 0) & (c < cols))
        def _():
            @pl.when(s > 0)
            def _():
                arrive(k, i, c)

            onward_on(way, i, c, start)

            @pl.when(s > 0)
            def _():
                @pl.when(i == z)
                def _():
                    ship_on(c, start)

                partner_on(i, c, start)

    def step(n):
        @pl.loop(0, cols)
        def _(s):
            stream(0, cols - 1 - n, s)
            stream(1, n, s)

    def relay_on(c, act):
        @pl.when(relays_up)
        def _():
            act(relay(0, c), 1)

        @pl.when(relays_down)
        def _():
            act(relay(1, c), 0)

    def receive_and_relay(c):
        def act(copy, way):
            taken(way, c)
            copy.start()

        relay_on(c, act)

    def relay_all():
        receive_and_relay(z)

        @pl.loop(1, cols)
        def _(s):
            @pl.when(z - s >= 0)
            def _():
                receive_and_relay(z - s)

            @pl.when(z + s < cols)
            def _():
                receive_and_relay(z + s)

    def scale(way, source):
        @pl.loop(0, cols)
        def _(c):
            wgt[way, c] = (source(c).astype(jnp.float32) * occ_ref[c]).astype(jnp.bfloat16)

    def prepare():
        for way, present, waited in ((0, lower, relays_down), (1, upper, relays_up)):

            @pl.when(present)
            def _():
                @pl.when(jnp.logical_not(waited))
                def _():
                    @pl.loop(0, cols)
                    def _(c):
                        taken(way, c)

                scale(way, lambda c: raw[way, c])

        scale(2, lambda c: gat[k, z, c])

    def answer(t):
        low = t < place
        other = jnp.where(low, t, t + 1)
        slot = jnp.where(low, size + other - place, other - place - size) + W - 1
        near = (slot >= 0) & (slot < 2 * W - 1)
        return low, other, slot, near

    def reply(t):
        low, other, slot, near = answer(t)
        there = lax.rem(jnp.where(low, row - per, row + per) + rows, rows)
        go = near & jnp.where(low, row - per >= 0, row + per < rows)
        slot = jnp.clip(slot, 0, 2 * W - 2)
        return go, remote(res.at[t], out_ref.at[slot], osem.at[t], qsem.at[slot], (there, z))

    def local(t):
        other = t - (size - 1)
        slot = other - place + W - 1
        near = (slot >= 0) & (slot < 2 * W - 1)
        slot = jnp.clip(slot, 0, 2 * W - 2)
        return near, pltpu.make_async_copy(res.at[t], out_ref.at[slot], osem.at[t])

    def product(t, way, other):
        kk, i = other // cols, lax.rem(other, cols)
        total = jnp.zeros(res.shape[1:], jnp.float32)
        for c in range(cols):
            total = total + lax.dot_general(
                wgt[way, c], gat[kk, i, c], (((1,), (1,)), ((), ())), preferred_element_type=jnp.float32
            )
        res[t] = total.astype(jnp.bfloat16)

    def home(other):
        t = other + size - 1
        near, copy = local(t)

        @pl.when(near)
        def _():
            product(t, 2, other)
            copy.start()

    def away(other):
        low = other < place
        t = jnp.clip(jnp.where(low, other, other - 1), 0, size - 2)
        go, copy = reply(t)

        @pl.when(go & (other != place))
        def _():
            product(t, jnp.where(low, 0, 1), other)
            copy.start()

    def work(i):
        for d in range(1, per):
            kk = lax.rem(k + d, per)

            @pl.loop(0, cols)
            def _(c):
                arrive(kk, i, c)

        @pl.loop(0, per)
        def _(kk):
            away(kk * cols + i)

        @pl.when(edge)
        def _():
            @pl.loop(0, per)
            def _(kk):
                home(kk * cols + i)

    relay_at = jnp.where(edge, 0, jnp.maximum(z, cols - 1 - z))
    ready_at = jnp.where(edge, 0, cols - 1)

    ship_on(z, start)

    @pl.loop(0, cols)
    def _(n):
        step(n)

        @pl.when(n == 0)
        def _():
            @pl.loop(0, cols)
            def _(i):
                partner_on(i, z, start)

        @pl.when(n == relay_at)
        def _():
            relay_all()

        @pl.when(n == ready_at)
        def _():
            prepare()

        @pl.when(n >= ready_at)
        def _():
            @pl.loop(0, cols)
            def _(i):
                whole = jnp.where(z == 0, i, jnp.where(z == cols - 1, cols - 1 - i, jnp.maximum(i, cols - 1 - i)))

                @pl.when((whole == n) | ((n == ready_at) & (whole < n)))
                def _():
                    work(i)

    @pl.when(jnp.logical_not(edge))
    def _():
        @pl.loop(0, size)
        def _(other):
            home(other)

    @pl.loop(0, cols)
    def _(c):
        ship_on(c, sent)
        relay_on(c, lambda copy, way: sent(copy))

        @pl.loop(0, cols)
        def _(i):
            onward_on(0, i, c, sent)
            onward_on(1, i, c, sent)
            partner_on(i, c, sent)

    @pl.loop(0, size - 1)
    def _(t):
        go, copy = reply(t)

        @pl.when(go)
        def _():
            copy.wait_send()

        low, other, slot, near = answer(t)
        due = near & jnp.where(low, row + per < rows, row - per >= 0)
        slot = jnp.clip(slot, 0, 2 * W - 2)

        @pl.when(due)
        def _():
            remote(res.at[t], out_ref.at[slot], osem.at[t], qsem.at[slot], (row, z)).wait_recv()

    @pl.loop(size - 1, 2 * size - 1)
    def _(t):
        near, copy = local(t)

        @pl.when(near)
        def _():
            copy.wait()


def place_blocks(neighbours_ref, counts_ref, block_ref, out_ref, held, blank, in_sem, out_sem):
    here = lax.axis_index("row") * lax.axis_size("col") + lax.axis_index("col")
    blank[...] = jnp.zeros_like(blank)

    def fetch(j):
        at = jnp.clip(neighbours_ref[0, j] - here + (W - 1), 0, 2 * W - 2)
        return pltpu.make_async_copy(block_ref.at[at], held.at[j], in_sem.at[j])

    def store(j, source):
        return pltpu.make_async_copy(source, out_ref.at[j], out_sem.at[j])

    slots = out_ref.shape[0]
    for j in range(slots):

        @pl.when(j < counts_ref[0])
        def _():
            fetch(j).start()

        @pl.when(j >= counts_ref[0])
        def _():
            store(j, blank).start()

    for j in range(slots):

        @pl.when(j < counts_ref[0])
        def _():
            fetch(j).wait()
            store(j, held.at[j]).start()

    for j in range(slots):
        store(j, blank).wait()


def shards(coeffs, occupations, block_order, neighbours, counts):
    rows, cols = lax.axis_size("row"), lax.axis_size("col")
    states = coeffs.shape[1]
    depth = coeffs.shape[0] // cols
    per = -(-W // cols)
    size = per * cols
    slots_total = 2 * W - 1
    first = lax.axis_index("row") * cols
    picks = lax.dynamic_slice_in_dim(block_order, first, cols) - first
    own = coeffs.reshape(cols, depth, states)[picks]
    occ = occupations.reshape(cols, 1, states)
    dma = pltpu.SemaphoreType.DMA
    blocks = pl.pallas_call(
        functools.partial(kernel, rows, cols, per),
        out_shape=jax.ShapeDtypeStruct((slots_total, depth, depth), jnp.bfloat16),
        in_specs=[pl.BlockSpec(memory_space=pl.ANY), pl.BlockSpec(memory_space=pltpu.VMEM)],
        out_specs=pl.BlockSpec(memory_space=pl.ANY),
        scratch_shapes=[
            pltpu.VMEM((per, cols, cols, depth, states), jnp.bfloat16),
            pltpu.VMEM((2, cols, depth, states), jnp.bfloat16),
            pltpu.VMEM((3, cols, depth, states), jnp.bfloat16),
            pltpu.VMEM((2 * size - 1, depth, depth), jnp.bfloat16),
            dma,
            dma((2, cols, cols)),
            dma((max(per - 1, 1), cols, cols)),
            dma((per, cols, cols)),
            dma((2, cols)),
            dma((cols,)),
            dma((2, cols)),
            dma((2 * size - 1,)),
            dma((slots_total,)),
        ],
        compiler_params=pltpu.CompilerParams(
            collective_id=0, has_side_effects=True, vmem_limit_bytes=60 * 1024 * 1024
        ),
        name="density_blocks",
    )(own, occ)
    slots = neighbours.shape[1]
    placed = pl.pallas_call(
        place_blocks,
        out_shape=jax.ShapeDtypeStruct((slots, depth, depth), jnp.bfloat16),
        in_specs=[
            pl.BlockSpec(memory_space=pltpu.SMEM),
            pl.BlockSpec(memory_space=pltpu.SMEM),
            pl.BlockSpec(memory_space=pl.ANY),
        ],
        out_specs=pl.BlockSpec(memory_space=pl.ANY),
        scratch_shapes=[
            pltpu.VMEM((slots, depth, depth), jnp.bfloat16),
            pltpu.VMEM((depth, depth), jnp.bfloat16),
            dma((slots,)),
            dma((slots,)),
        ],
        name="place_blocks",
    )(neighbours, counts, blocks)
    return placed[None]


def solution(mesh):
    return jax.shard_map(
        shards,
        mesh=mesh,
        in_specs=(P("row", "col"), P(), P(), P(("row", "col"), None), P(("row", "col"))),
        out_specs=P(("row", "col"), None, None, None),
        check_vma=False,
    )
```

```python
import functools

import jax
import jax.numpy as jnp
from jax import lax
from jax.experimental import pallas as pl
from jax.experimental.pallas import tpu as pltpu
from jax.sharding import PartitionSpec as P

W = 8
LAG = 1
MESH = pl.DeviceIdType.MESH


def kernel(rows, cols, per, own_ref, occ_ref, out_ref, gat, raw, wgt, res, in_sem, dsem, fsem, psem, rsem, xsem, ysem, usem, osem, qsem):
    row, z = lax.axis_index("row"), lax.axis_index("col")
    k = lax.rem(row, per)
    base = row - k
    place = k * cols + z
    size = per * cols
    has_up, has_down = row + per < rows, row >= per
    has_up2, has_down2 = row + 2 * per < rows, row >= 2 * per
    odd = lax.rem(row // per, 2) == 1
    ships_up = has_up & jnp.logical_not(odd) & ((place > 0) | has_down)
    ships_down = has_down & jnp.where(odd, (place < size - 1) | has_up, (place < size - 1) & jnp.logical_not(has_up))
    relays_up = has_up2 & (place > 0) & jnp.logical_not(odd)
    relays_down = has_down2 & (place < size - 1) & odd
    lower, upper = has_down & (place > 0), has_up & (place < size - 1)
    edge = (z == 0) | (z == cols - 1)

    def remote(src, dst, send, recv, device):
        return pltpu.make_async_remote_copy(
            src_ref=src, dst_ref=dst, send_sem=send, recv_sem=recv, device_id=device, device_id_type=MESH
        )

    def direct(i):
        return remote(gat.at[k, i, z], gat.at[k, i, z], dsem.at[i], rsem.at[k, i, z], (row, i))

    def onward(way, i, c):
        step = 1 - 2 * way
        there = lax.rem(z + step + cols, cols)
        return remote(gat.at[k, i, c], gat.at[k, i, c], fsem.at[way, i, c], rsem.at[k, i, c], (row, there))

    def partner(d, i, c):
        there = base + lax.rem(k + d, per)
        return remote(gat.at[k, i, c], gat.at[k, i, c], psem.at[d - 1, i, c], rsem.at[k, i, c], (there, z))

    def ship(way, c):
        there = lax.rem(row + (1 - 2 * way) * per + rows, rows)
        return remote(gat.at[k, z, c], raw.at[way, c], xsem.at[way, c], usem.at[way, c], (there, z))

    def relay(way, c):
        there = lax.rem(row + (2 - 4 * way) * per + 2 * rows, rows)
        return remote(raw.at[1 - way, c], raw.at[way, c], ysem.at[c], usem.at[way, c], (there, z))

    def taken(way, c):
        remote(raw.at[way, c], raw.at[way, c], xsem.at[0, 0], usem.at[way, c], (row, z)).wait_recv()

    def arrive(kk, i, c):
        remote(gat.at[kk, i, c], gat.at[kk, i, c], dsem.at[0], rsem.at[kk, i, c], (row, z)).wait_recv()

    def pass_on(i, c, act):
        @pl.when((c <= z) & (z < cols - 1) & (i != z + 1))
        def _():
            act(onward(0, i, c))

        @pl.when((c >= z) & (z > 0) & (i != z - 1))
        def _():
            act(onward(1, i, c))

        for d in range(1, per):
            act(partner(d, i, c))

    def ship_on(c, act):
        @pl.when(ships_up)
        def _():
            act(ship(0, c))

        @pl.when(ships_down)
        def _():
            act(ship(1, c))

    def start(copy):
        copy.start()

    def sent(copy):
        copy.wait_send()

    fill = pltpu.make_async_copy(own_ref, gat.at[k, :, z], in_sem)
    fill.start()
    barrier = pltpu.get_barrier_semaphore()
    for d in range(1, cols):
        pl.semaphore_signal(barrier, inc=1, device_id=(row, lax.rem(z + d, cols)), device_id_type=MESH)
    for d in range(1, per):
        pl.semaphore_signal(barrier, inc=1, device_id=(base + lax.rem(k + d, per), z), device_id_type=MESH)

    greeted = cols + per - 2
    for present, step in ((has_up, per), (has_down, -per), (has_up2, 2 * per), (has_down2, -2 * per)):
        greeted = greeted + present.astype(jnp.int32)

        @pl.when(present)
        def _():
            there = lax.rem(row + step + 2 * rows, rows)
            pl.semaphore_signal(barrier, inc=1, device_id=(there, z), device_id_type=MESH)

    pl.semaphore_wait(barrier, greeted)
    fill.wait()

    for d in range(1, cols):
        direct(lax.rem(z + d, cols)).start()
    ship_on(z, start)

    @pl.loop(0, cols)
    def _(i):
        pass_on(i, z, start)

    def sides(s, act):
        @pl.when(z - s >= 0)
        def _():
            act(z - s)

        @pl.when(z + s < cols)
        def _():
            act(z + s)

    @pl.loop(1, cols)
    def _(s):
        def act(c):
            arrive(k, z, c)
            ship_on(c, start)
            pass_on(z, c, start)

        sides(s, act)

    def relay_on(c, act):
        @pl.when(relays_up)
        def _():
            act(relay(0, c), 1)

        @pl.when(relays_down)
        def _():
            act(relay(1, c), 0)

    def receive_and_relay(c):
        def act(copy, way):
            taken(way, c)
            copy.start()

        relay_on(c, act)

    receive_and_relay(z)

    @pl.loop(1, cols)
    def _(s):
        sides(s, receive_and_relay)

    def scale(way, source):
        @pl.loop(0, cols)
        def _(c):
            wgt[way, c] = (source(c).astype(jnp.float32) * occ_ref[c]).astype(jnp.bfloat16)

    def prepare():
        for way, present, waited in ((0, lower, relays_down), (1, upper, relays_up)):

            @pl.when(present)
            def _():
                @pl.when(jnp.logical_not(waited))
                def _():
                    @pl.loop(0, cols)
                    def _(c):
                        taken(way, c)

                scale(way, lambda c: raw[way, c])

        scale(2, lambda c: gat[k, z, c])

    def answer(t):
        low = t < place
        other = jnp.where(low, t, t + 1)
        slot = jnp.where(low, size + other - place, other - place - size) + W - 1
        near = (slot >= 0) & (slot < 2 * W - 1)
        return low, other, slot, near

    def reply(t):
        low, other, slot, near = answer(t)
        there = lax.rem(jnp.where(low, row - per, row + per) + rows, rows)
        go = near & jnp.where(low, row - per >= 0, row + per < rows)
        slot = jnp.clip(slot, 0, 2 * W - 2)
        return go, remote(res.at[t], out_ref.at[slot], osem.at[t], qsem.at[slot], (there, z))

    def local(t):
        other = t - (size - 1)
        slot = other - place + W - 1
        near = (slot >= 0) & (slot < 2 * W - 1)
        slot = jnp.clip(slot, 0, 2 * W - 2)
        return near, pltpu.make_async_copy(res.at[t], out_ref.at[slot], osem.at[t])

    def product(t, way, other):
        kk, i = other // cols, lax.rem(other, cols)
        total = jnp.zeros(res.shape[1:], jnp.float32)
        for c in range(cols):
            total = total + lax.dot_general(
                wgt[way, c], gat[kk, i, c], (((1,), (1,)), ((), ())), preferred_element_type=jnp.float32
            )
        res[t] = total.astype(jnp.bfloat16)

    def home(other):
        t = other + size - 1
        near, copy = local(t)

        @pl.when(near)
        def _():
            product(t, 2, other)
            copy.start()

    def away(other):
        low = other < place
        t = jnp.clip(jnp.where(low, other, other - 1), 0, size - 2)
        go, copy = reply(t)

        @pl.when(go & (other != place))
        def _():
            product(t, jnp.where(low, 0, 1), other)
            copy.start()

    def work(q):
        i = jnp.where(q == 0, z, jnp.where(q - 1 < z, q - 1, q))
        for d in range(1, per):
            kk = lax.rem(k + d, per)

            @pl.loop(0, cols)
            def _(c):
                arrive(kk, i, c)

        @pl.loop(0, per)
        def _(kk):
            away(kk * cols + i)

        @pl.when(edge)
        def _():
            @pl.loop(0, per)
            def _(kk):
                home(kk * cols + i)

    lag = jnp.where(edge, 0, LAG)

    @pl.loop(0, cols + LAG)
    def _(n):
        @pl.when((n >= 1) & (n < cols))
        def _():
            i = jnp.where(n - 1 < z, n - 1, n)

            @pl.loop(1, cols)
            def _(s):
                def act(c):
                    arrive(k, i, c)
                    pass_on(i, c, start)

                sides(s, act)

        q = n - lag

        @pl.when(q == 0)
        def _():
            prepare()

        @pl.when((q >= 0) & (q < cols))
        def _():
            work(q)

    @pl.when(jnp.logical_not(edge))
    def _():
        @pl.loop(0, size)
        def _(other):
            home(other)

    for d in range(1, cols):
        direct(lax.rem(z + d, cols)).wait_send()

    @pl.loop(0, cols)
    def _(c):
        ship_on(c, sent)
        relay_on(c, lambda copy, way: sent(copy))

        @pl.loop(0, cols)
        def _(i):
            pass_on(i, c, sent)

    @pl.loop(0, size - 1)
    def _(t):
        go, copy = reply(t)

        @pl.when(go)
        def _():
            copy.wait_send()

        low, other, slot, near = answer(t)
        due = near & jnp.where(low, row + per < rows, row - per >= 0)
        slot = jnp.clip(slot, 0, 2 * W - 2)

        @pl.when(due)
        def _():
            remote(res.at[t], out_ref.at[slot], osem.at[t], qsem.at[slot], (row, z)).wait_recv()

    @pl.loop(size - 1, 2 * size - 1)
    def _(t):
        near, copy = local(t)

        @pl.when(near)
        def _():
            copy.wait()


def place_blocks(neighbours_ref, counts_ref, block_ref, out_ref, held, blank, in_sem, out_sem):
    here = lax.axis_index("row") * lax.axis_size("col") + lax.axis_index("col")
    blank[...] = jnp.zeros_like(blank)

    def fetch(j):
        at = jnp.clip(neighbours_ref[0, j] - here + (W - 1), 0, 2 * W - 2)
        return pltpu.make_async_copy(block_ref.at[at], held.at[j], in_sem.at[j])

    def store(j, source):
        return pltpu.make_async_copy(source, out_ref.at[j], out_sem.at[j])

    slots = out_ref.shape[0]
    for j in range(slots):

        @pl.when(j < counts_ref[0])
        def _():
            fetch(j).start()

        @pl.when(j >= counts_ref[0])
        def _():
            store(j, blank).start()

    for j in range(slots):

        @pl.when(j < counts_ref[0])
        def _():
            fetch(j).wait()
            store(j, held.at[j]).start()

    for j in range(slots):
        store(j, blank).wait()


def shards(coeffs, occupations, block_order, neighbours, counts):
    rows, cols = lax.axis_size("row"), lax.axis_size("col")
    states = coeffs.shape[1]
    depth = coeffs.shape[0] // cols
    per = -(-W // cols)
    size = per * cols
    slots_total = 2 * W - 1
    first = lax.axis_index("row") * cols
    picks = lax.dynamic_slice_in_dim(block_order, first, cols) - first
    own = coeffs.reshape(cols, depth, states)[picks]
    occ = occupations.reshape(cols, 1, states)
    dma = pltpu.SemaphoreType.DMA
    blocks = pl.pallas_call(
        functools.partial(kernel, rows, cols, per),
        out_shape=jax.ShapeDtypeStruct((slots_total, depth, depth), jnp.bfloat16),
        in_specs=[pl.BlockSpec(memory_space=pl.ANY), pl.BlockSpec(memory_space=pltpu.VMEM)],
        out_specs=pl.BlockSpec(memory_space=pl.ANY),
        scratch_shapes=[
            pltpu.VMEM((per, cols, cols, depth, states), jnp.bfloat16),
            pltpu.VMEM((2, cols, depth, states), jnp.bfloat16),
            pltpu.VMEM((3, cols, depth, states), jnp.bfloat16),
            pltpu.VMEM((2 * size - 1, depth, depth), jnp.bfloat16),
            dma,
            dma((cols,)),
            dma((2, cols, cols)),
            dma((max(per - 1, 1), cols, cols)),
            dma((per, cols, cols)),
            dma((2, cols)),
            dma((cols,)),
            dma((2, cols)),
            dma((2 * size - 1,)),
            dma((slots_total,)),
        ],
        compiler_params=pltpu.CompilerParams(
            collective_id=0, has_side_effects=True, vmem_limit_bytes=60 * 1024 * 1024
        ),
        name="density_blocks",
    )(own, occ)
    slots = neighbours.shape[1]
    placed = pl.pallas_call(
        place_blocks,
        out_shape=jax.ShapeDtypeStruct((slots, depth, depth), jnp.bfloat16),
        in_specs=[
            pl.BlockSpec(memory_space=pltpu.SMEM),
            pl.BlockSpec(memory_space=pltpu.SMEM),
            pl.BlockSpec(memory_space=pl.ANY),
        ],
        out_specs=pl.BlockSpec(memory_space=pl.ANY),
        scratch_shapes=[
            pltpu.VMEM((slots, depth, depth), jnp.bfloat16),
            pltpu.VMEM((depth, depth), jnp.bfloat16),
            dma((slots,)),
            dma((slots,)),
        ],
        name="place_blocks",
    )(neighbours, counts, blocks)
    return placed[None]


def solution(mesh):
    return jax.shard_map(
        shards,
        mesh=mesh,
        in_specs=(P("row", "col"), P(), P(), P(("row", "col"), None), P(("row", "col"))),
        out_specs=P(("row", "col"), None, None, None),
        check_vma=False,
    )
```
